768 devices in a mesh: cells: 768 (over y, z, x, core).
Axes of the slice: x: 4, y: 8, z: 12, core: 2. Of those that a mesh axis runs over, the one named last changes fastest.
Arguments:
- block: bfloat16 [165888, 128], P('cells'), may hold values from -6 to 6
- cell_matrix: bfloat16 [768, 343, 343], P('cells'), may hold values from -1 to 3
- connectivity: int32 [768, 343], P('cells'), may hold values from 0 to 342, as said below
- potential: float32 [263424], P('cells'), may hold values from -1.5 to 1.5
- locked: bfloat16 [165888, 704], P('cells'), may hold values from -0.015625 to 0.015625
Outputs:
- filtered: bfloat16 [165888, 128], P('cells')
- intersection: float32 [704, 128], replicated
The draws below stay inside these ranges and needn't reach their ends.
Inputs may be any that keep to these rules, and one draw needn't show every extreme that they name: `connectivity`: A partition's 1 row list each of its 1 x 1 x 1 cells once, in some order; a row gives the local slots of that sixth-order hexahedron's 343 nodes, in some order, where a node with local coordinates (i, j, k), each from 0 to 6, has slot (i * 7 + j) * 7 + k; neighbouring cells share nodes.
All inputs are finite; a program needn't handle non-finite values.
Results may differ from the reference program's by a relative error of at most 0.0067.
Values may be sent and summed in bfloat16 or wider, within the bound.
A program may use at most 32 MiB of HBM per device.

```python
import math
import jax
import jax.numpy as jnp
from jax import lax

NPC = 343
STATES = 128
LOCKED = 704
CB = 1
GRID_Y = 4
GRID_Z = 4
CELLS_DEV = 1
SIDE = 7
NODE_DEV = 343
ALL_CELLS = 768
NODES = 165888
SLOTS = 263424
N_CELLS = 768


def draw_cell_matrix(key, part):
    key_offdiag = jax.random.fold_in(key, 11)
    key_diagonal = jax.random.fold_in(key, 12)
    spread = 0.6 / math.sqrt(NPC)
    offdiag = jnp.clip(jax.random.normal(key_offdiag, (ALL_CELLS, NPC, NPC), jnp.float32), -6.0, 6.0) * spread
    diagonal = jax.random.uniform(key_diagonal, (ALL_CELLS, NPC), jnp.float32, 0.5, 1.5)
    identity = jnp.eye(NPC, dtype=jnp.float32)
    return (offdiag + diagonal[:, :, None] * identity).astype(jnp.bfloat16)


def node_order(order_key):
    return jax.random.permutation(order_key, NPC).astype(jnp.int32)


def draw_connectivity(key, part):
    within = jnp.arange(NPC, dtype=jnp.int32)
    node_u = within // 49
    node_v = within // 7 % 7
    node_w = within % 7
    cell_ids = jnp.arange(CELLS_DEV, dtype=jnp.int32)
    cell_a = cell_ids // (CB * CB)
    cell_b = cell_ids // CB % CB
    cell_c = cell_ids % CB
    slot_table = ((6 * cell_a[:, None] + node_u[None, :]) * SIDE + 6 * cell_b[:, None] + node_v[None, :]) * SIDE + 6 * cell_c[:, None] + node_w[None, :]

    def one_part(part_key):
        cell_order = jax.random.permutation(jax.random.fold_in(part_key, 1), CELLS_DEV).astype(jnp.int32)
        orders = jax.vmap(node_order)(jax.random.split(jax.random.fold_in(part_key, 2), CELLS_DEV))
        chosen = jnp.take(slot_table, cell_order, axis=0)
        return jnp.take_along_axis(chosen, orders, axis=1)
    part_keys = jax.random.split(jax.random.fold_in(key, 21), ALL_CELLS // CELLS_DEV)
    return jax.vmap(one_part)(part_keys).reshape(ALL_CELLS, NPC).astype(jnp.int32)


def steps_of(stream_key, shape, shards, low, largest):
    def one(axis_at, shards_of):
        heights = jax.random.uniform(jax.random.fold_in(jax.random.fold_in(stream_key, 6), axis_at), (shards_of,), jnp.float32, low / len(shards), largest / len(shards))
        return jnp.repeat(jnp.exp(heights), shape[axis_at] // shards_of).reshape((-1,) + (1,) * (len(shape) - axis_at - 1))

    gain = one(*shards[0])
    for cut in shards[1:]:
        gain = gain * one(*cut)
    return gain


def centred(stream_key, shape, scale, limit, cuts=(), kind=jnp.bfloat16):
    entries = jax.random.normal(stream_key, shape, jnp.float32) * scale
    if len(cuts) > 0:
        entries = steps_of(stream_key, shape, cuts, -0.22, 0.18) * entries
    return jnp.clip(entries, min=-limit, max=limit).astype(kind)


def setup_inputs(seed: int = 0) -> dict:
    streams_of = jax.random.split(jax.random.key(seed), 6)
    block = centred(streams_of[0], (NODES, STATES), 1.0, 6.0, ((0, 768),))
    cell_matrix = draw_cell_matrix(jax.random.fold_in(streams_of[5], 71), 0)
    connectivity = draw_connectivity(jax.random.fold_in(streams_of[5], 71), 0)
    potential = jnp.clip(jax.random.uniform(streams_of[3], (SLOTS,), jnp.float32, -1.5, 1.5) * steps_of(streams_of[3], (SLOTS,), ((0, 768),), -0.4, 0.0), -1.5, 1.5)
    locked = centred(streams_of[4], (NODES, LOCKED), NODES ** -0.5, 0.015625, ((0, 768),))
    return {"block": block, "cell_matrix": cell_matrix, "connectivity": connectivity, "potential": potential, "locked": locked}


chebyshev_coeffs = ((-1.0 / 7.0, 0.0), (-7.0 / 41.0, 8.0 / 41.0), (-41.0 / 259.0, 28.0 / 259.0))
centre = 6.0


def cell_terms(local_rows, matrices, links, lumped):
    gathered = jnp.take(local_rows, links, axis=0).astype(jnp.float32)
    products = jnp.einsum("cij,cjs->cis", matrices.astype(jnp.float32), gathered)
    summed = jnp.zeros((NODE_DEV, STATES), jnp.float32).at[links.reshape(-1)].add(products.reshape(-1, STATES))
    return summed + lumped[:, None] * local_rows.astype(jnp.float32)


def advance(applied, previous, older, coeffs):
    return (coeffs[0] * (applied - centre * previous.astype(jnp.float32)) - coeffs[1] * older.astype(jnp.float32)).astype(jnp.bfloat16)


def reference(block, cell_matrix, connectivity, potential, locked):
    edge = 6 * CB
    grid_x = N_CELLS // (GRID_Y * GRID_Z)
    matrices = cell_matrix.reshape(N_CELLS, CELLS_DEV, NPC, NPC)
    links = connectivity.reshape(N_CELLS, CELLS_DEV, NPC)
    lumped = potential.reshape(N_CELLS, NODE_DEV)
    window = (SIDE, SIDE, SIDE, STATES)

    def apply_operator(states):
        grid = states.reshape(grid_x, GRID_Y, GRID_Z, edge, edge, edge, STATES)
        grid = grid.transpose(0, 3, 1, 4, 2, 5, 6).reshape(grid_x * edge, GRID_Y * edge, GRID_Z * edge, STATES)
        padded = jnp.pad(grid, ((1, 0), (1, 0), (1, 0), (0, 0)))

        def one_part(index, total):
            part = jnp.asarray(index).astype(jnp.int32)
            part_x = part // (GRID_Y * GRID_Z)
            part_y = (part // GRID_Z) % GRID_Y
            part_z = part % GRID_Z
            start = (part_x * edge, part_y * edge, part_z * edge, jnp.zeros((), jnp.int32))
            local_rows = lax.dynamic_slice(padded, start, window).reshape(NODE_DEV, STATES)
            partial_value = cell_terms(local_rows, matrices[part], links[part], lumped[part])
            updated = lax.dynamic_slice(total, start, window) + partial_value.reshape(window)
            return lax.dynamic_update_slice(total, updated, start)

        total = lax.fori_loop(0, N_CELLS, one_part, jnp.zeros(padded.shape, jnp.float32))
        owned = total[1:, 1:, 1:].reshape(grid_x, edge, GRID_Y, edge, GRID_Z, edge, STATES)
        return owned.transpose(0, 2, 4, 1, 3, 5, 6).reshape(NODES, STATES)

    older = block
    current = block
    for coeffs in chebyshev_coeffs:
        following = advance(apply_operator(current), current, older, coeffs)
        older = current
        current = following
    filtered = current
    intersection = jnp.einsum("nl,ns->ls", locked.astype(jnp.float32), filtered.astype(jnp.float32))
    return filtered, intersection
```

```python
import itertools

import jax
import jax.numpy as jnp
import numpy as np
from jax import lax
from jax.experimental import pallas as pl
from jax.experimental.pallas import tpu as pltpu
from jax.sharding import PartitionSpec as P

GRID = (48, 4, 4)
SIDE = 7
NPC = 343
NP = 384
OWNED = 216
STATES = 128
LOCKED = 704
LPAD = 768
CENTRE = 6.0
COEFFS = ((-1.0 / 7.0, 0.0), (-7.0 / 41.0, 8.0 / 41.0), (-41.0 / 259.0, 28.0 / 259.0))
F32, BF16, I32 = jnp.float32, jnp.bfloat16, jnp.int32
MESH = pl.DeviceIdType.MESH

RING_G, RING_Z, RING_Y = 8, 12, 8
ROWS_G = LPAD // RING_G
OWNERS = 6
ROWS_Y = ROWS_G // OWNERS


def neighbour_blocks():
    every = [o for o in itertools.product((-1, 0, 1), repeat=3) if any(o)]
    faces_first = sorted(every, key=lambda o: sum(map(abs, o)))
    upper = [o for o in faces_first if min(o) >= 0]
    lower = [o for o in faces_first if max(o) <= 0]
    mixed = [o for o in faces_first if min(o) < 0 < max(o)]
    blocks, start = [], 0
    for offset in upper + lower + mixed:
        size = 64 if sum(map(abs, offset)) == 1 else 16
        blocks.append((offset, start, size))
        start += size
    return blocks, start


BLOCKS, ROWS = neighbour_blocks()
UPPER, LOWER = BLOCKS[:7], BLOCKS[7:14]
HALF = 256


def tables():
    pick = np.zeros((ROWS, NP), np.float32)
    where_to = np.zeros((8, ROWS), np.int32)
    where_to[0] = -1
    for offset, start, size in BLOCKS:
        ranges = [{1: (6,), 0: range(SIDE), -1: (0,)}[c] for c in offset]
        for row, node in enumerate(itertools.product(*ranges)):
            i, j, k = node
            pick[start + row, (i * SIDE + j) * SIDE + k] = 1.0
            i, j, k = (n - 6 * c for n, c in zip(node, offset))
            where_to[0, start + row] = (i * SIDE + j) * SIDE + k
        for c in range(3):
            where_to[1 + c, start : start + size] = offset[c]
    return pick, where_to


PICK, WHERE_TO = tables()


def dot(a, b):
    return jnp.dot(a, b, preferred_element_type=F32)


def dot_nt(a, b):
    return lax.dot_general(a, b, (((1,), (1,)), ((), ())), preferred_element_type=F32)


def one_hot(a, b):
    return jnp.where(a == b, 1.0, 0.0).astype(BF16)


def split(n, by):
    q = jnp.floor((n + 0.5) * (1.0 / by))
    return q, n - q * by


def owned_slot(n):
    i, rest = split(n, 36)
    j, k = split(rest, 6)
    return (i + 1.0) * 49.0 + (j + 1.0) * 7.0 + (k + 1.0)


def fiota(shape, dim):
    return lax.broadcasted_iota(I32, shape, dim).astype(F32)


def kernel(
    block_ref, a_ref, conn_ref, pot_ref, locked_ref, pick_ref, where_ref,
    filt_ref, inter_ref,
    mext, mloc, smat, potp, lpad, lown, llt,
    snd0, rcv0, sndl, rcvl, snd1, rcv1, snd2, rcv2, snd3, rcv3,
    buf1, rc1, tot2, buf2, rc2, rc3, buf4, rc5,
    hs, hr, s1, r1, s2, r2, s3, r3, s4, r4, s5, r5,
):
    me = lax.axis_index("cells")
    pos = (me // 16, (me // 4) % 4, me % 4)
    g = me % 8
    z = (me // 8) % 12
    y = me // 96

    def at(offset):
        px, py, pz = ((p + c + n) % n for p, c, n in zip(pos, offset, GRID))
        return px * 16 + py * 4 + pz

    def at_g(d):
        return me - g + (g + d) % RING_G

    def at_z(d):
        return me + 8 * ((z + d) % RING_Z - z)

    def at_y(d):
        return me + 96 * ((y + d) % RING_Y - y)

    barrier = pltpu.get_barrier_semaphore()
    partners = [at(o) for o, _, _ in BLOCKS]
    partners += [at_g(d) for d in range(1, RING_G)]
    partners += [at_z(d) for d in range(1, RING_Z)]
    partners += [at_y(d) for d in range(1, RING_Y)]
    for partner in partners:
        pl.semaphore_signal(barrier, inc=1, device_id=(partner,), device_id_type=MESH)

    def remote(src, dst, send, recv, device):
        return pltpu.make_async_remote_copy(
            src_ref=src, dst_ref=dst, send_sem=send, recv_sem=recv,
            device_id=(device,), device_id_type=MESH,
        )

    def send_blocks(blocks, base, snd, rcv, at_sem):
        for offset, start, size in blocks[::-1]:
            rows = pl.ds(start - base, size)
            remote(snd.at[rows], rcv.at[rows], hs.at[at_sem], hr.at[at_sem], at(offset)).start()

    def whole(snd, rcv, at_sem):
        return remote(snd, rcv, hs.at[at_sem], hr.at[at_sem], at(BLOCKS[0][0]))

    place = one_hot(fiota((NP, OWNED), 0), owned_slot(fiota((NP, OWNED), 1)))
    y_own = dot(place, block_ref[...])
    pick_up = pick_ref[0:HALF, :]
    snd0[...] = dot(pick_up, y_own.astype(BF16)).astype(BF16)
    lpad[:, LOCKED - 64 : LPAD] = jnp.zeros((OWNED, 128), BF16)
    lpad[:, 0:LOCKED] = locked_ref[...]
    lown[...] = dot(place, lpad[...]).astype(BF16)
    sndl[...] = dot(pick_up, lown[...]).astype(BF16)
    pl.semaphore_wait(barrier, len(partners))
    send_blocks(UPPER, 0, snd0, rcv0, 0)
    send_blocks(UPPER, 0, sndl, rcvl, 1)

    ct = one_hot(lax.broadcasted_iota(I32, (NP, NPC), 0), conn_ref[...])
    rows_in_order = dot(ct, a_ref[...]).astype(BF16)
    potp[...] = jnp.zeros_like(potp)
    potp[0:1, 0:NPC] = pot_ref[...]
    on_diagonal = lax.broadcasted_iota(I32, (NP, NP), 0) == lax.broadcasted_iota(I32, (NP, NP), 1)
    full = dot_nt(rows_in_order, ct) + jnp.where(on_diagonal, potp[0:1, :], 0.0)
    rounded = full.astype(BF16)
    mloc[...] = rounded
    lost = jnp.sum(full - rounded.astype(F32), axis=1, keepdims=True)
    mext[...] = dot(pick_ref[...], mloc[...]).astype(BF16)

    slot = where_ref[0:1, :]
    for c in range(3):
        source = pos[c] - where_ref[1 + c : 2 + c, :]
        slot = jnp.where(source < 0, -1, jnp.where(source >= GRID[c], -1, slot))
    smat[...] = one_hot(lax.broadcasted_iota(I32, (NP, ROWS), 0), slot)

    node = fiota((NP, STATES), 0)
    i, rest = split(node, 49)
    j, k = split(rest, 7)
    inside = jnp.where(node < NPC - 0.5, 1.0, 0.0)
    owned = inside
    for local, p in zip((i, j, k), pos):
        inside = jnp.where(local + (6 * p).astype(F32) < 0.5, 0.0, inside)
        owned = jnp.where(local < 0.5, 0.0, owned)

    whole(snd0, rcv0, 0).wait_recv()
    current = (y_own + dot(smat[:, 0:HALF], rcv0[...])).astype(BF16)
    older = current
    for step, (snd, rcv) in enumerate(((snd1, rcv1), (snd2, rcv2))):
        c, d = COEFFS[step]
        snd[...] = dot(mext[...], current).astype(BF16)
        send_blocks(BLOCKS, 0, snd, rcv, 2 + step)
        here = dot(mloc[...], current) + (lost - CENTRE) * current.astype(F32)
        if step == 0:
            whole(sndl, rcvl, 1).wait_recv()
            local_locked = lown[...].astype(F32) + dot(smat[:, 0:HALF], rcvl[...])
            llt[...] = local_locked.T.astype(BF16)
        whole(snd, rcv, 2 + step).wait_recv()
        applied = here + dot(smat[...], rcv[...])
        following = (inside * (c * applied - d * older.astype(F32))).astype(BF16)
        older = current
        current = following

    c, d = COEFFS[2]
    third, second = current.astype(F32), older.astype(F32)
    here = dot(mloc[...], current) + lost * third
    own_terms = owned * (c * CENTRE * third + d * second)
    share = dot(llt[...], (c * here - own_terms).astype(BF16))
    buf1[...] = share.astype(BF16).reshape(RING_G, ROWS_G, STATES)
    for dist in range(1, RING_G):
        remote(
            buf1.at[(g + dist) % RING_G], rc1.at[dist - 1], s1.at[dist - 1], r1.at[dist - 1], at_g(dist)
        ).start()

    snd3[...] = dot(mext[HALF : 2 * HALF, :], current).astype(BF16)
    send_blocks(LOWER, HALF, snd3, rcv3, 4)

    acc = buf1[g].astype(F32)
    for dist in range(1, RING_G):
        remote(buf1.at[0], rc1.at[dist - 1], s1.at[dist - 1], r1.at[dist - 1], at_g(dist)).wait_recv()
        acc = acc + rc1[dist - 1].astype(F32)
    tot2[...] = acc.reshape(OWNERS, ROWS_Y, STATES)
    buf2[...] = acc.astype(BF16).reshape(OWNERS, ROWS_Y, STATES)

    def copy2(dist):
        to = (y + dist) % RING_Y
        return remote(
            buf2.at[jnp.minimum(to, OWNERS - 1)], rc2.at[dist - 1], s2.at[dist - 1], r2.at[dist - 1], at_y(dist)
        )

    for dist in range(1, RING_Y):
        @pl.when((y + dist) % RING_Y < OWNERS)
        def _():
            copy2(dist).start()

    whole(snd3, rcv3, 4).wait_recv()
    applied = here + dot(smat[:, HALF : 2 * HALF], rcv3[...])
    result = (c * (applied - CENTRE * third) - d * second).astype(BF16)
    take = one_hot(fiota((OWNED, NP), 1), owned_slot(fiota((OWNED, NP), 0)))
    filt_ref[...] = dot(take, result).astype(BF16)

    def copy3(dist):
        return remote(rc3.at[0], rc3.at[dist], s3.at[dist - 1], r3.at[dist - 1], at_z(dist))

    def copy4(dist, back=0):
        row = jnp.minimum((y - back + RING_Y) % RING_Y, OWNERS - 1)
        return remote(buf4.at[row], buf4.at[row], s4.at[dist - 1], r4.at[dist - 1], at_y(dist))

    @pl.when(y < OWNERS)
    def _():
        acc = tot2[jnp.minimum(y, OWNERS - 1)]
        for dist in range(1, RING_Y):
            copy2(dist).wait_recv()
            acc = acc + rc2[dist - 1].astype(F32)
        rc3[0] = acc.astype(BF16)
        for dist in range(1, RING_Z):
            copy3(dist).start()
        for dist in range(1, RING_Z):
            copy3(dist).wait_recv()
        total = rc3[z % RING_Z].astype(F32)
        for row in range(1, RING_Z):
            total = total + rc3[(z - row + RING_Z) % RING_Z].astype(F32)
        buf4[jnp.minimum(y, OWNERS - 1)] = total.astype(BF16)
        for dist in range(1, RING_Y):
            copy4(dist).start()

    for dist in range(1, RING_Y):
        @pl.when((y - dist + RING_Y) % RING_Y < OWNERS)
        def _():
            copy4(dist, dist).wait_recv()

    rc5[g] = buf4[...].reshape(ROWS_G, STATES)

    def copy5(dist, back=0):
        row = (g - back + RING_G) % RING_G
        return remote(rc5.at[row], rc5.at[row], s5.at[dist - 1], r5.at[dist - 1], at_g(dist))

    for dist in range(1, RING_G):
        copy5(dist).start()
    for dist in range(1, RING_G):
        copy5(dist, dist).wait_recv()
    inter_ref[...] = rc5[...].reshape(LPAD, STATES)[0:LOCKED, :]

    whole(snd0, rcv0, 0).wait_send()
    whole(sndl, rcvl, 1).wait_send()
    whole(snd1, rcv1, 2).wait_send()
    whole(snd2, rcv2, 3).wait_send()
    whole(snd3, rcv3, 4).wait_send()
    for dist in range(1, RING_G):
        remote(buf1.at[0], rc1.at[dist - 1], s1.at[dist - 1], r1.at[dist - 1], at_g(dist)).wait_send()
        copy5(dist).wait_send()
    for dist in range(1, RING_Y):
        @pl.when((y + dist) % RING_Y < OWNERS)
        def _():
            copy2(dist).wait_send()

    @pl.when(y < OWNERS)
    def _():
        for dist in range(1, RING_Z):
            copy3(dist).wait_send()
        for dist in range(1, RING_Y):
            copy4(dist).wait_send()


def per_device(block, cell_matrix, connectivity, potential, locked):
    vmem = pl.BlockSpec(memory_space=pltpu.VMEM)
    scratch = [
        ((ROWS, NP), BF16), ((NP, NP), BF16), ((NP, ROWS), BF16), ((8, NP), F32),
        ((OWNED, LPAD), BF16), ((NP, LPAD), BF16), ((LPAD, NP), BF16),
        ((HALF, STATES), BF16), ((HALF, STATES), BF16),
        ((HALF, LPAD), BF16), ((HALF, LPAD), BF16),
        ((ROWS, STATES), BF16), ((ROWS, STATES), BF16),
        ((ROWS, STATES), BF16), ((ROWS, STATES), BF16),
        ((HALF, STATES), BF16), ((HALF, STATES), BF16),
        ((RING_G, ROWS_G, STATES), BF16), ((RING_G - 1, ROWS_G, STATES), BF16),
        ((OWNERS, ROWS_Y, STATES), F32), ((OWNERS, ROWS_Y, STATES), BF16),
        ((RING_Y - 1, ROWS_Y, STATES), BF16), ((RING_Z, ROWS_Y, STATES), BF16),
        ((OWNERS, ROWS_Y, STATES), BF16), ((RING_G, ROWS_G, STATES), BF16),
    ]
    sems = (5, 5, 7, 7, 7, 7, 11, 11, 7, 7, 7, 7)
    filtered, intersection = pl.pallas_call(
        kernel,
        out_shape=(
            jax.ShapeDtypeStruct((OWNED, STATES), BF16),
            jax.ShapeDtypeStruct((LOCKED, STATES), BF16),
        ),
        in_specs=[vmem] * 7,
        out_specs=(vmem, vmem),
        scratch_shapes=[pltpu.VMEM(*s) for s in scratch] + [pltpu.SemaphoreType.DMA((n,)) for n in sems],
        compiler_params=pltpu.CompilerParams(
            collective_id=0, has_side_effects=True, vmem_limit_bytes=48 << 20
        ),
        name="filter",
    )(
        block, cell_matrix.reshape(NPC, NPC), connectivity.reshape(1, NPC), potential.reshape(1, NPC), locked,
        jnp.asarray(PICK, BF16), jnp.asarray(WHERE_TO),
    )
    return filtered, intersection.astype(F32)


def solution(mesh):
    in_specs = (
        P("cells", None),
        P("cells", None, None),
        P("cells", None),
        P("cells"),
        P("cells", None),
    )
    out_specs = (P("cells", None), P())
    return jax.shard_map(
        per_device, mesh=mesh, in_specs=in_specs, out_specs=out_specs, check_vma=False
    )
```
